32 devices in a mesh: section: 4 (over x, core), seq: 8 (over z, y).
Axes of the slice: x: 2, y: 2, z: 4, core: 2. Of those that a mesh axis runs over, the one named last changes fastest.
Arguments:
- layer_input: bfloat16 [4, 512, 4, 1536], P('section', 'seq'), may hold values from -300 to 300
- norm_gain: float32 [4, 1536], P('section'), may hold values from 0.1 to 1.9
- queries: bfloat16 [4, 512, 4, 1024], P('section', 'seq'), may hold values from -6 to 6
- key_states: bfloat16 [4, 512, 4, 1024], P('section', 'seq'), may hold values from -6 to 6
- value_states: bfloat16 [4, 512, 4, 1024], P('section', 'seq'), may hold values from -6 to 6
- out_grad: bfloat16 [4, 512, 4, 1536], P('section', 'seq'), may hold values from -6 to 6
- out_weight: bfloat16 [4, 1024, 1536], P('section', 'seq'), may hold values from -0.1875 to 0.1875
- qkv_weight: bfloat16 [4, 1536, 3072], P('section', 'seq'), may hold values from -0.15625 to 0.15625
- lengths: int32 [4, 4], P('section'), may hold values from 256 to 512
Outputs:
- passed_grad: bfloat16 [4, 512, 4, 1536], P('section', 'seq')
The draws below stay inside these ranges and needn't reach their ends.
All inputs are finite; a program needn't handle non-finite values.
Results may differ from the reference program's by a relative error of at most 0.0034.
Values may be sent and summed in bfloat16 or wider, within the bound.
A program may use at most 128 MiB of HBM per device.

```python
import jax
import jax.numpy as jnp
from jax import lax

D = 1536
HEADS = 16
HS = 64
SEQS = 4
SECTIONS = 4
L = 512


def draw_queries(key, part):
    values = jnp.clip(1.5 * jax.random.normal(jax.random.fold_in(key, 21), (SECTIONS, L, SEQS, HEADS * HS), jnp.float32), -6.0, 6.0)
    return values.astype(jnp.bfloat16)


def draw_key_states(key, part):
    values = jnp.clip(1.5 * jax.random.normal(jax.random.fold_in(key, 22), (SECTIONS, L, SEQS, HEADS * HS), jnp.float32), -6.0, 6.0)
    return values.astype(jnp.bfloat16)


def draw_layer_input(key, part):
    values = jnp.clip(jax.random.normal(jax.random.fold_in(key, 31), (SECTIONS, L, SEQS, D), jnp.float32), -6.0, 6.0)
    return values.astype(jnp.bfloat16)


def with_ends(values, stream_key, least, high):
    spot = [jax.random.randint(jax.random.fold_in(stream_key, axis), (), 0, length) for axis, length in enumerate(values.shape)]
    widest = values.shape.index(max(values.shape))
    next_to = spot[:widest] + [(spot[widest] + 1) % values.shape[widest]] + spot[widest + 1:]
    return values.at[tuple(spot)].set(least).at[tuple(next_to)].set(high)


def steps_of(stream_key, extent, cuts, least, high):
    level = 1.0
    for axis_at, blocks in cuts:
        draws = jax.random.uniform(jax.random.fold_in(jax.random.fold_in(stream_key, 6), axis_at), (blocks,), jnp.float32, least / len(cuts), high / len(cuts))
        level = level * jnp.repeat(jnp.exp(draws), extent[axis_at] // blocks).reshape((-1,) + (1,) * (len(extent) - 1 - axis_at))
    return level


def gaussian(rng, extent, scale, bound, shards=(), held_as=jnp.bfloat16):
    entries = jax.random.normal(rng, extent, jnp.float32) * scale
    if len(shards) > 0:
        entries = steps_of(rng, extent, shards, -0.22, 0.18) * entries
    return jnp.clip(entries, min=-bound, max=bound).astype(held_as)


def setup_inputs(seed: int = 0) -> dict:
    splits = jax.random.split(jax.random.key(seed), 10)
    return {
        "layer_input": draw_layer_input(jax.random.fold_in(splits[9], 71), 0),
        "norm_gain": jnp.clip(1.0 + 0.18 * jax.random.normal(splits[1], (SECTIONS, D), jnp.float32), 0.1, 1.9),
        "queries": draw_queries(jax.random.fold_in(splits[9], 71), 0),
        "key_states": draw_key_states(jax.random.fold_in(splits[9], 71), 0),
        "value_states": gaussian(splits[4], (SECTIONS, L, SEQS, HEADS * HS), 1.0, 6.0, ((0, 4), (1, 8))),
        "out_grad": gaussian(splits[5], (SECTIONS, L, SEQS, D), 1.0, 6.0, ((0, 4), (1, 8))),
        "out_weight": gaussian(splits[6], (SECTIONS, HEADS * HS, D), (HEADS * HS) ** -0.5, 0.1875, ((0, 4), (1, 8))),
        "qkv_weight": gaussian(splits[7], (SECTIONS, D, 3 * HEADS * HS), D ** -0.5, 0.15625, ((0, 4), (1, 8))),
        "lengths": with_ends(jax.random.randint(splits[8], (SECTIONS, SEQS), L // 2, L + 1), jax.random.fold_in(splits[8], 1), L // 2, L).astype(jnp.int32),
    }


EPSILON = 1e-05
MASKED = -1e+30

def item_backward(query_rows, key_rows, value_rows, grad_rows, key_valid):
    length = query_rows.shape[0]
    block = min(512, length)
    scale = HS ** (-0.5)
    offsets = jnp.arange(0, length, block).astype(jnp.int32)
    zeros = jnp.zeros((length, query_rows.shape[1]), jnp.float32)

    def step(carry, offset):
        key_total, value_total = carry
        query_block = lax.dynamic_slice_in_dim(query_rows, offset, block, 0)
        grad_block = lax.dynamic_slice_in_dim(grad_rows, offset, block, 0)
        scores = jnp.dot(query_block, key_rows.T, preferred_element_type=jnp.float32) * scale
        scores = jnp.where(key_valid[None, :], scores, MASKED)
        largest = lax.optimization_barrier(jnp.max(scores, axis=1, keepdims=True))
        weights = jnp.exp(scores - largest)
        probs = weights / lax.optimization_barrier(jnp.sum(weights, axis=1, keepdims=True))
        probs_low = probs.astype(jnp.bfloat16)
        grad_probs = jnp.dot(grad_block, value_rows.T, preferred_element_type=jnp.float32)
        centre = lax.optimization_barrier(jnp.sum(probs * grad_probs, axis=1, keepdims=True))
        grad_scores = (probs * (grad_probs - centre) * scale).astype(jnp.bfloat16)
        query_grad = jnp.dot(grad_scores, key_rows, preferred_element_type=jnp.float32)
        key_total = key_total + jnp.dot(grad_scores.T, query_block, preferred_element_type=jnp.float32)
        value_total = value_total + jnp.dot(probs_low.T, grad_block, preferred_element_type=jnp.float32)
        return ((key_total, value_total), query_grad.astype(jnp.bfloat16))
    (key_total, value_total), query_parts = lax.scan(step, (zeros, zeros), offsets)
    query_grad = query_parts.reshape(length, query_rows.shape[1])
    return (query_grad, key_total.astype(jnp.bfloat16), value_total.astype(jnp.bfloat16))

def to_items(array):
    return array.reshape(L, SEQS, HEADS, HS).transpose(1, 2, 0, 3).reshape(SEQS * HEADS, L, HS)

def from_items(array):
    return array.reshape(SEQS, HEADS, L, HS).transpose(2, 0, 1, 3).reshape(L * SEQS, HEADS * HS)

def section_backward(operands):
    layer_input, norm_gain, queries, key_states, value_states, out_grad, out_weight, qkv_weight, lengths = operands
    flat_grad = out_grad.reshape(L * SEQS, D)
    attn_grad = jnp.dot(flat_grad, out_weight.T, preferred_element_type=jnp.float32).astype(jnp.bfloat16)
    attn_grad = attn_grad.reshape(L, SEQS, HEADS * HS)
    positions = jnp.arange(L).astype(jnp.int32)
    valid = positions[None, :] < lengths[:, None]
    valid_items = jnp.repeat(valid, HEADS, axis=0)
    query_grad, key_gradient, value_grad = lax.map(lambda group: item_backward(*group), (to_items(queries), to_items(key_states), to_items(value_states), to_items(attn_grad), valid_items))
    joined = jnp.concatenate([from_items(query_grad), from_items(key_gradient), from_items(value_grad)], axis=1)
    norm_grad = jnp.dot(joined, qkv_weight.T, preferred_element_type=jnp.float32)
    inputs = layer_input.reshape(L * SEQS, D).astype(jnp.float32)
    row_average = lax.optimization_barrier(jnp.mean(inputs, axis=1, keepdims=True))
    centered_input = inputs - row_average
    var = lax.optimization_barrier(jnp.mean(centered_input * centered_input, axis=1, keepdims=True))
    inverse_deviation = 1.0 / jnp.sqrt(var + EPSILON)
    normalized_input = centered_input * inverse_deviation
    scaled_rows = norm_grad * norm_gain[None, :]
    residual_branch = inverse_deviation * (scaled_rows - lax.optimization_barrier(jnp.mean(scaled_rows, axis=1, keepdims=True)) - normalized_input * lax.optimization_barrier(jnp.mean(scaled_rows * normalized_input, axis=1, keepdims=True)))
    input_grad = (flat_grad.astype(jnp.float32) + residual_branch).astype(jnp.bfloat16)
    return input_grad.reshape(L, SEQS, D)

def reference(layer_input, norm_gain, queries, key_states, value_states, out_grad, out_weight, qkv_weight, lengths):
    input_grad = lax.map(section_backward, (layer_input, norm_gain, queries, key_states, value_states, out_grad, out_weight, qkv_weight, lengths))
    return jnp.roll(input_grad, -1, axis=0)
```

```python
import functools

import jax
import jax.numpy as jnp
from jax import lax
from jax.experimental import pallas as pl
from jax.experimental.pallas import tpu as pltpu
from jax.sharding import PartitionSpec as P

HEADS = 16
HS = 64


EPSILON = 1e-05
MASKED = -1e30
ROW_DOT = (((1,), (1,)), ((), ()))
COL_DOT = (((0,), (0,)), ((), ()))


def shifted(shard, axis, by):
    count = lax.axis_size(axis)
    return lax.ppermute(shard, axis, [(i, (i + by) % count) for i in range(count)])


def item_backward(query_rows, key_rows, value_rows, grad_rows, key_valid):
    length = query_rows.shape[0]
    block = min(512, length)
    scale = HS ** (-0.5)
    offsets = jnp.arange(0, length, block)
    zeros = jnp.zeros((length, query_rows.shape[1]), jnp.float32)

    def step(carry, offset):
        key_total, value_total = carry
        query_block = lax.dynamic_slice_in_dim(query_rows, offset, block, 0)
        grad_block = lax.dynamic_slice_in_dim(grad_rows, offset, block, 0)
        scores = (
            lax.dot_general(query_block, key_rows, ROW_DOT, preferred_element_type=jnp.float32)
            * scale
        )
        scores = jnp.where(key_valid[None, :], scores, MASKED)
        largest = jnp.max(scores, axis=1, keepdims=True)
        weights = jnp.exp(scores - largest)
        probs = weights / jnp.sum(weights, axis=1, keepdims=True)
        probs_low = probs.astype(jnp.bfloat16)
        grad_probs = lax.dot_general(
            grad_block, value_rows, ROW_DOT, preferred_element_type=jnp.float32
        )
        centre = jnp.sum(probs * grad_probs, axis=1, keepdims=True)
        grad_scores = (probs * (grad_probs - centre) * scale).astype(jnp.bfloat16)
        query_grad = jnp.dot(grad_scores, key_rows, preferred_element_type=jnp.float32)
        key_total = key_total + lax.dot_general(
            grad_scores, query_block, COL_DOT, preferred_element_type=jnp.float32
        )
        value_total = value_total + lax.dot_general(
            probs_low, grad_block, COL_DOT, preferred_element_type=jnp.float32
        )
        return ((key_total, value_total), query_grad.astype(jnp.bfloat16))

    (key_total, value_total), query_parts = lax.scan(step, (zeros, zeros), offsets)
    query_grad = query_parts.reshape(length, query_rows.shape[1])
    return (query_grad, key_total.astype(jnp.bfloat16), value_total.astype(jnp.bfloat16))


def split_items(columns):
    length = columns.shape[0]
    count = columns.shape[1] // HS
    return columns.reshape(length, count, HS).transpose(1, 0, 2)


def join_items(items):
    count = items.shape[0]
    length = items.shape[1]
    return items.transpose(1, 0, 2).reshape(length, count * HS)


def project_grad(flat_grad, out_rows):
    return lax.dot_general(
        flat_grad,
        lax.all_gather(out_rows, "seq", axis=0, tiled=True),
        ROW_DOT,
        preferred_element_type=jnp.float32,
    ).astype(jnp.bfloat16)


def on_device(
    layer_input,
    norm_gain,
    queries,
    key_states,
    value_states,
    out_grad,
    out_weight,
    qkv_weight,
    lengths,
):
    frames = queries.shape[1]
    records = queries.shape[2]
    features = queries.shape[3]
    model_width = out_grad.shape[3]
    flat_grad = out_grad[0].reshape(frames * records, model_width)
    frame_queries = queries[0].reshape(frames, records * features)
    frame_keys = key_states[0].reshape(frames, records * features)
    frame_values = value_states[0].reshape(frames, records * features)
    attn_grad = project_grad(flat_grad, out_weight[0])
    head_queries, head_keys, head_values, head_grads = (
        lax.all_to_all(frame_queries, "seq", split_axis=1, concat_axis=0, tiled=True),
        lax.all_to_all(frame_keys, "seq", split_axis=1, concat_axis=0, tiled=True),
        lax.all_to_all(frame_values, "seq", split_axis=1, concat_axis=0, tiled=True),
        lax.all_to_all(
            attn_grad.reshape(frames, records * features),
            "seq",
            split_axis=1,
            concat_axis=0,
            tiled=True,
        ),
    )
    items_here = head_queries.shape[1] // HS
    length = head_queries.shape[0]
    item_ids = lax.axis_index("seq") * items_here + jnp.arange(items_here, dtype=jnp.int32)
    record_ids = item_ids // HEADS
    record_pick = jnp.arange(records, dtype=jnp.int32)[None, :] == record_ids[:, None]
    item_lengths = jnp.sum(jnp.where(record_pick, lengths[0][None, :], 0), axis=1)
    key_valid = jnp.arange(length, dtype=jnp.int32)[None, :] < item_lengths[:, None]
    query_grad, key_gradient, value_grad = lax.map(
        lambda group: item_backward(*group),
        (
            split_items(head_queries),
            split_items(head_keys),
            split_items(head_values),
            split_items(head_grads),
            key_valid,
        ),
    )
    query_back, key_backward, value_back = (
        lax.all_to_all(join_items(query_grad), "seq", split_axis=0, concat_axis=1, tiled=True),
        lax.all_to_all(join_items(key_gradient), "seq", split_axis=0, concat_axis=1, tiled=True),
        lax.all_to_all(join_items(value_grad), "seq", split_axis=0, concat_axis=1, tiled=True),
    )
    joined = jnp.concatenate(
        [
            query_back.reshape(frames * records, features),
            key_backward.reshape(frames * records, features),
            value_back.reshape(frames * records, features),
        ],
        axis=1,
    )
    norm_grad = lax.dot_general(
        joined,
        lax.all_gather(qkv_weight[0], "seq", axis=0, tiled=True),
        ROW_DOT,
        preferred_element_type=jnp.float32,
    )
    inputs = layer_input[0].reshape(frames * records, model_width).astype(jnp.float32)
    row_average = jnp.mean(inputs, axis=1, keepdims=True)
    centered_input = inputs - row_average
    var = jnp.mean(centered_input * centered_input, axis=1, keepdims=True)
    inverse_deviation = 1.0 / jnp.sqrt(var + EPSILON)
    normalized_input = centered_input * inverse_deviation
    scaled_rows = norm_grad * norm_gain[0][None, :]
    residual_branch = inverse_deviation * (
        scaled_rows
        - jnp.mean(scaled_rows, axis=1, keepdims=True)
        - normalized_input * jnp.mean(scaled_rows * normalized_input, axis=1, keepdims=True)
    )
    input_grad = (flat_grad.astype(jnp.float32) + residual_branch).astype(jnp.bfloat16)
    input_grad = input_grad.reshape(1, frames, records, model_width)
    return shifted(input_grad, "section", -1)


def body(
    dims,
    length_ref,
    li_ref,
    q_ref,
    k_ref,
    v_ref,
    og_ref,
    ow_in,
    w_in,
    gain_ref,
    out_ref,
    xq,
    xk,
    xv,
    xg,
    g_send,
    ow,
    w,
    joined,
    part_send,
    part_recv,
    li_here,
    og_here,
    x_send_sem,
    x_recv_sem,
    ow_send_sem,
    ow_side_sem,
    ow_recv_sem,
    w_send_sem,
    w_side_sem,
    w_recv_sem,
    p_send_sem,
    p_recv_sem,
    s_send_sem,
    s_recv_sem,
    local_sem,
):
    n, sections, groups, parts, frames, cols = dims
    pairs = cols // (2 * HS)
    section = lax.axis_index("section")
    me = lax.axis_index("seq")
    group = me // parts
    part = me % parts
    before = (section + sections - 1) % sections
    after = (section + 1) % sections

    def remote(src, dst, send, recv, sec, dev):
        return pltpu.make_async_remote_copy(
            src_ref=src,
            dst_ref=dst,
            send_sem=send,
            recv_sem=recv,
            device_id=(sec, dev),
            device_id_type=pl.DeviceIdType.MESH,
        )

    barrier = pltpu.get_barrier_semaphore()

    def greet(sec, dev):
        pl.semaphore_signal(
            barrier, inc=1, device_id=(sec, dev), device_id_type=pl.DeviceIdType.MESH
        )

    for k in range(1, n):
        greet(section, (me + k) % n)
    for k in range(n):
        greet(before, (me + k) % n)
        greet(after, (me + k) % n)

    heads = [(q_ref, xq), (k_ref, xk), (v_ref, xv), (g_send, xg)]

    def own(t):
        src, dst = heads[t]
        return pltpu.make_async_copy(
            src.at[group, :, pl.ds(pl.multiple_of(part * cols, cols), cols)],
            dst.at[me],
            local_sem.at[t],
        )

    def exchange(t, k):
        src, dst = heads[t]
        to = (me + k) % n
        return remote(
            src.at[to // parts, :, pl.ds(pl.multiple_of((to % parts) * cols, cols), cols)],
            dst.at[me],
            x_send_sem.at[t, k],
            x_recv_sem.at[t, k],
            section,
            to,
        )

    local_ow = pltpu.make_async_copy(ow_in, ow.at[me], local_sem.at[4])
    local_w = pltpu.make_async_copy(w_in.at[part], w.at[me], local_sem.at[5])
    local_ow.start()
    local_w.start()
    for t in range(3):
        own(t).start()
    pl.semaphore_wait(barrier, 3 * n - 1)
    local_ow.wait()

    def ow_hop(slot, way, dev):
        return remote(
            ow.at[slot], ow.at[slot], ow_send_sem.at[way, slot], ow_recv_sem.at[slot], section, dev
        )

    def ow_side(slot, k):
        return remote(
            ow.at[slot],
            ow.at[slot],
            ow_side_sem.at[k, slot],
            ow_recv_sem.at[slot],
            section,
            group * parts + (part + k) % parts,
        )

    def w_hop(slot, way, dev):
        return remote(
            w.at[slot], w.at[slot], w_send_sem.at[way, slot], w_recv_sem.at[slot], section, dev
        )

    def w_side(k):
        other = (part + k) % parts
        return remote(
            w_in.at[other],
            w.at[me],
            w_side_sem.at[k],
            w_recv_sem.at[me],
            section,
            group * parts + other,
        )

    def ways(origin, act):
        @pl.when((origin <= group) & (group + 1 < groups))
        def _():
            act(0, me + parts)

        @pl.when((origin >= group) & (group >= 1))
        def _():
            act(1, me - parts)

    def ow_pass(origin):
        slot = origin * parts + part
        ways(origin, lambda way, dev: ow_hop(slot, way, dev).start())
        for k in range(1, parts):
            ow_side(slot, k).start()

    def ow_arrive(origin):
        @pl.when((origin >= 0) & (origin < groups))
        def _():
            slot = origin * parts + part
            ow_hop(slot, 0, me).wait_recv()
            ow_pass(origin)

    def w_pass(origin):
        @pl.when((origin >= 0) & (origin < groups))
        def _():
            for other in range(parts):
                slot = origin * parts + other

                @pl.when(slot != me)
                def _():
                    w_hop(slot, 0, me).wait_recv()

                ways(origin, lambda way, dev: w_hop(slot, way, dev).start())

    ow_pass(group)
    shift_og = remote(og_ref, og_here, s_send_sem.at[0], s_recv_sem.at[0], before, me)
    shift_li = remote(li_ref, li_here, s_send_sem.at[1], s_recv_sem.at[1], before, me)
    for k in range(1, n):
        exchange(0, k).start()
    shift_og.start()
    shift_li.start()
    for s in range(1, groups):
        ow_arrive(group - s)
        ow_arrive(group + s)
        if s == 1:
            for t in (1, 2):
                for k in range(1, n):
                    exchange(t, k).start()
    for k in range(1, parts):
        w_side(k).start()
    for origin in range(groups):
        for k in range(1, parts):
            ow_side(origin * parts + (part + k) % parts, k).wait_recv()

    features = groups * parts
    rows_here = ow.shape[1]

    def project(i, carry):
        weight = ow[pl.ds(2 * i, 2)].reshape(2 * rows_here, ow.shape[2])
        result = lax.dot_general(
            og_ref[...], weight, ROW_DOT, preferred_element_type=jnp.float32
        ).astype(jnp.bfloat16)
        g_send[:, :, pl.ds(pl.multiple_of(i * 2 * rows_here, 2 * rows_here), 2 * rows_here)] = (
            result.reshape(groups, frames, 2 * rows_here)
        )
        return carry

    lax.fori_loop(0, features // 2, project, 0)
    own(3).start()
    for k in range(1, n):
        exchange(3, k).start()
    local_w.wait()
    w_pass(group)
    for t in range(4):
        own(t).wait()
        for k in range(1, n):
            exchange(t, k).wait_recv()

    length = n * frames
    valid = length_ref[0]
    keys_ok = lax.broadcasted_iota(jnp.int32, (length, 1), 0) < valid
    low_lanes = lax.broadcasted_iota(jnp.int32, (length, 2 * HS), 1) < HS
    scale = HS ** (-0.5)

    def attend(j, carry):
        lanes = pl.ds(pl.multiple_of(j * 2 * HS, 2 * HS), 2 * HS)
        queries, keys, values, grads = (
            x[:, :, lanes].reshape(length, 2 * HS) for x in (xq, xk, xv, xg)
        )
        keys_across = keys.T
        nothing = jnp.zeros_like(keys)
        halves = []
        for h in range(2):
            mine = low_lanes if h == 0 else jnp.logical_not(low_lanes)
            key_h = jnp.where(mine, keys, nothing)
            value_h = jnp.where(mine, values, nothing)
            scores = (
                lax.dot_general(key_h, queries, ROW_DOT, preferred_element_type=jnp.float32)
                * scale
            )
            scores = jnp.where(keys_ok, scores, MASKED)
            weights = jnp.exp(scores - jnp.max(scores, axis=0, keepdims=True))
            probs = weights * (1.0 / jnp.sum(weights, axis=0, keepdims=True))
            grad_probs = lax.dot_general(
                value_h, grads, ROW_DOT, preferred_element_type=jnp.float32
            )
            centre = jnp.sum(probs * grad_probs, axis=0, keepdims=True)
            grad_scores = (probs * (grad_probs - centre)).astype(jnp.bfloat16)
            value_grad = jnp.dot(
                probs.astype(jnp.bfloat16), grads, preferred_element_type=jnp.float32
            )
            key_grad = jnp.dot(grad_scores, queries, preferred_element_type=jnp.float32)
            query_grad = jnp.dot(
                keys_across[h * HS : (h + 1) * HS], grad_scores, preferred_element_type=jnp.float32
            )
            halves.append((query_grad, key_grad, value_grad))
        (query_0, key_0, value_0), (query_1, key_1, value_1) = halves
        query_both = (jnp.concatenate([query_0, query_1], axis=0) * scale).T
        key_both = jnp.where(low_lanes, key_0, key_1) * scale
        value_both = jnp.where(low_lanes, value_0, value_1)
        for t, both in enumerate((query_both, key_both, value_both)):
            at = pl.multiple_of(t * cols + j * 2 * HS, 2 * HS)
            joined[:, pl.ds(at, 2 * HS)] = both.astype(jnp.bfloat16)

        @pl.when(j == pairs - 2)
        def _():
            w_pass(group - 1)
            w_pass(group + 1)

        return carry

    if pairs < 2:
        w_pass(group - 1)
        w_pass(group + 1)
    lax.fori_loop(0, pairs, attend, 0)

    def part_copy(origin, to):
        return remote(
            part_send.at[origin, to],
            part_recv.at[me, origin],
            p_send_sem.at[origin, to],
            p_recv_sem.at[me, origin],
            before,
            to,
        )

    def norm_block(i, carry):
        s = (i + 1) // 2
        origin = group + s * (1 - 2 * (i % 2))

        @pl.when(i >= 3)
        def _():
            w_pass(origin)

        @pl.when((origin >= 0) & (origin < groups))
        def _():
            weight = w[pl.ds(origin * parts, parts)].reshape(parts * w.shape[1], w.shape[2])
            sums = lax.dot_general(
                joined[...], weight, ROW_DOT, preferred_element_type=jnp.float32
            )
            sums = (sums * gain_ref[origin]).astype(jnp.bfloat16)
            part_send[origin] = sums.reshape(n, frames, sums.shape[1])
            for k in range(n):
                part_copy(origin, (me + k) % n).start()

        return carry

    lax.fori_loop(0, 2 * groups - 1, norm_block, 0)

    shift_og.wait_recv()
    shift_li.wait_recv()
    for src in range(n):
        for origin in range(groups):
            remote(
                part_send.at[origin, 0],
                part_recv.at[src, origin],
                p_send_sem.at[origin, 0],
                p_recv_sem.at[src, origin],
                before,
                me,
            ).wait_recv()

    width = li_here.shape[1]
    block = part_recv.shape[3]

    def finish(r, carry):
        rows = pl.ds(pl.multiple_of(r * frames, frames), frames)
        inputs = li_here[rows, :].astype(jnp.float32)
        centered = inputs - jnp.sum(inputs, axis=1, keepdims=True) * (1.0 / width)
        var = jnp.sum(centered * centered, axis=1, keepdims=True) * (1.0 / width)
        deviation = 1.0 / jnp.sqrt(var + EPSILON)
        normal = centered * deviation
        scaled = []
        for origin in range(groups):
            total = part_recv[r * parts, origin].astype(jnp.float32)
            for k in range(1, parts):
                total = total + part_recv[r * parts + k, origin].astype(jnp.float32)
            scaled.append(total)
        scaled = jnp.concatenate(scaled, axis=1)
        average = jnp.sum(scaled, axis=1, keepdims=True) * (1.0 / width)
        along = jnp.sum(scaled * normal, axis=1, keepdims=True) * (1.0 / width)
        branch = deviation * (scaled - average - normal * along)
        out_ref[rows, :] = (og_here[rows, :].astype(jnp.float32) + branch).astype(jnp.bfloat16)
        return carry

    lax.fori_loop(0, groups, finish, 0)

    for t in range(4):
        for k in range(1, n):
            exchange(t, k).wait_send()
    for origin in range(groups):
        slot = origin * parts + part
        ways(origin, lambda way, dev: ow_hop(slot, way, dev).wait_send())
        for k in range(1, parts):
            ow_side(slot, k).wait_send()
        for other in range(parts):
            w_slot = origin * parts + other
            ways(origin, lambda way, dev: w_hop(w_slot, way, dev).wait_send())
        for to in range(n):
            part_copy(origin, to).wait_send()
    for k in range(1, parts):
        w_side(k).wait_send()
    shift_og.wait_send()
    shift_li.wait_send()


def on_device_fused(
    layer_input,
    norm_gain,
    queries,
    key_states,
    value_states,
    out_grad,
    out_weight,
    qkv_weight,
    lengths,
):
    n = lax.axis_size("seq")
    sections = lax.axis_size("section")
    frames, records, features = queries.shape[1:]
    width = out_grad.shape[3]
    parts = n // records
    cols = features // parts
    ow_rows = out_weight.shape[1]
    w_rows = qkv_weight.shape[1]
    block = parts * w_rows
    group = lax.axis_index("seq") // parts
    length_here = lax.dynamic_slice(lengths[0], (group,), (1,))

    def by_record(x):
        return x[0].transpose(1, 0, 2)

    flat_input = by_record(layer_input).reshape(records * frames, width)
    flat_grad = by_record(out_grad).reshape(records * frames, width)
    w_parts = (
        qkv_weight[0]
        .reshape(w_rows, 3, parts, cols)
        .transpose(2, 0, 1, 3)
        .reshape(parts, w_rows, 3 * cols)
    )
    gain = norm_gain[0].reshape(records, 1, block)
    vmem = pl.BlockSpec(memory_space=pltpu.VMEM)
    low = jnp.bfloat16
    dma = pltpu.SemaphoreType.DMA
    out = pl.pallas_call(
        functools.partial(body, (n, sections, records, parts, frames, cols)),
        out_shape=jax.ShapeDtypeStruct((records * frames, width), low),
        in_specs=[pl.BlockSpec(memory_space=pltpu.SMEM)] + [vmem] * 8,
        out_specs=vmem,
        scratch_shapes=[pltpu.VMEM((n, frames, cols), low)] * 4
        + [
            pltpu.VMEM((records, frames, features), low),
            pltpu.VMEM((n, ow_rows, width), low),
            pltpu.VMEM((n, w_rows, 3 * cols), low),
            pltpu.VMEM((n * frames, 3 * cols), low),
            pltpu.VMEM((records, n, frames, block), low),
            pltpu.VMEM((n, records, frames, block), low),
            pltpu.VMEM((records * frames, width), low),
            pltpu.VMEM((records * frames, width), low),
            dma((4, n)),
            dma((4, n)),
            dma((2, n)),
            dma((parts, n)),
            dma((n,)),
            dma((2, n)),
            dma((parts,)),
            dma((n,)),
            dma((records, n)),
            dma((n, records)),
            dma((2,)),
            dma((2,)),
            dma((6,)),
        ],
        compiler_params=pltpu.CompilerParams(
            collective_id=0, has_side_effects=True, vmem_limit_bytes=60 * 1024 * 1024
        ),
    )(
        length_here,
        flat_input,
        by_record(queries),
        by_record(key_states),
        by_record(value_states),
        flat_grad,
        out_weight[0],
        w_parts,
        gain,
    )
    return out.reshape(records, frames, width).transpose(1, 0, 2)[None]


def fits(mesh, records, features):
    n = mesh.shape["seq"]
    if n % records or mesh.shape["section"] < 2:
        return False
    parts = n // records
    return features % (parts * 2 * HS) == 0 and n % 2 == 0


def solution(mesh):
    in_specs = (
        P("section", "seq", None, None),
        P("section", None),
        P("section", "seq", None, None),
        P("section", "seq", None, None),
        P("section", "seq", None, None),
        P("section", "seq", None, None),
        P("section", "seq", None),
        P("section", "seq", None),
        P("section", None),
    )
    out_specs = P("section", "seq", None, None)

    def run(*arrays):
        fused = fits(mesh, arrays[2].shape[2], arrays[2].shape[3])
        return jax.shard_map(
            on_device_fused if fused else on_device,
            mesh=mesh,
            in_specs=in_specs,
            out_specs=out_specs,
            check_vma=False,
        )(*arrays)

    return run
```

```python
import functools

import jax
import jax.numpy as jnp
from jax import lax
from jax.experimental import pallas as pl
from jax.experimental.pallas import tpu as pltpu
from jax.sharding import PartitionSpec as P

HEADS = 16
HS = 64


EPSILON = 1e-05
MASKED = -1e30
ROW_DOT = (((1,), (1,)), ((), ()))
COL_DOT = (((0,), (0,)), ((), ()))


def shifted(shard, axis, by):
    count = lax.axis_size(axis)
    return lax.ppermute(shard, axis, [(i, (i + by) % count) for i in range(count)])


def item_backward(query_rows, key_rows, value_rows, grad_rows, key_valid):
    length = query_rows.shape[0]
    block = min(512, length)
    scale = HS ** (-0.5)
    offsets = jnp.arange(0, length, block)
    zeros = jnp.zeros((length, query_rows.shape[1]), jnp.float32)

    def step(carry, offset):
        key_total, value_total = carry
        query_block = lax.dynamic_slice_in_dim(query_rows, offset, block, 0)
        grad_block = lax.dynamic_slice_in_dim(grad_rows, offset, block, 0)
        scores = (
            lax.dot_general(query_block, key_rows, ROW_DOT, preferred_element_type=jnp.float32)
            * scale
        )
        scores = jnp.where(key_valid[None, :], scores, MASKED)
        largest = jnp.max(scores, axis=1, keepdims=True)
        weights = jnp.exp(scores - largest)
        probs = weights / jnp.sum(weights, axis=1, keepdims=True)
        probs_low = probs.astype(jnp.bfloat16)
        grad_probs = lax.dot_general(
            grad_block, value_rows, ROW_DOT, preferred_element_type=jnp.float32
        )
        centre = jnp.sum(probs * grad_probs, axis=1, keepdims=True)
        grad_scores = (probs * (grad_probs - centre) * scale).astype(jnp.bfloat16)
        query_grad = jnp.dot(grad_scores, key_rows, preferred_element_type=jnp.float32)
        key_total = key_total + lax.dot_general(
            grad_scores, query_block, COL_DOT, preferred_element_type=jnp.float32
        )
        value_total = value_total + lax.dot_general(
            probs_low, grad_block, COL_DOT, preferred_element_type=jnp.float32
        )
        return ((key_total, value_total), query_grad.astype(jnp.bfloat16))

    (key_total, value_total), query_parts = lax.scan(step, (zeros, zeros), offsets)
    query_grad = query_parts.reshape(length, query_rows.shape[1])
    return (query_grad, key_total.astype(jnp.bfloat16), value_total.astype(jnp.bfloat16))


def split_items(columns):
    length = columns.shape[0]
    count = columns.shape[1] // HS
    return columns.reshape(length, count, HS).transpose(1, 0, 2)


def join_items(items):
    count = items.shape[0]
    length = items.shape[1]
    return items.transpose(1, 0, 2).reshape(length, count * HS)


def project_grad(flat_grad, out_rows):
    return lax.dot_general(
        flat_grad,
        lax.all_gather(out_rows, "seq", axis=0, tiled=True),
        ROW_DOT,
        preferred_element_type=jnp.float32,
    ).astype(jnp.bfloat16)


def on_device(
    layer_input,
    norm_gain,
    queries,
    key_states,
    value_states,
    out_grad,
    out_weight,
    qkv_weight,
    lengths,
):
    frames = queries.shape[1]
    records = queries.shape[2]
    features = queries.shape[3]
    model_width = out_grad.shape[3]
    flat_grad = out_grad[0].reshape(frames * records, model_width)
    frame_queries = queries[0].reshape(frames, records * features)
    frame_keys = key_states[0].reshape(frames, records * features)
    frame_values = value_states[0].reshape(frames, records * features)
    attn_grad = project_grad(flat_grad, out_weight[0])
    head_queries, head_keys, head_values, head_grads = (
        lax.all_to_all(frame_queries, "seq", split_axis=1, concat_axis=0, tiled=True),
        lax.all_to_all(frame_keys, "seq", split_axis=1, concat_axis=0, tiled=True),
        lax.all_to_all(frame_values, "seq", split_axis=1, concat_axis=0, tiled=True),
        lax.all_to_all(
            attn_grad.reshape(frames, records * features),
            "seq",
            split_axis=1,
            concat_axis=0,
            tiled=True,
        ),
    )
    items_here = head_queries.shape[1] // HS
    length = head_queries.shape[0]
    item_ids = lax.axis_index("seq") * items_here + jnp.arange(items_here, dtype=jnp.int32)
    record_ids = item_ids // HEADS
    record_pick = jnp.arange(records, dtype=jnp.int32)[None, :] == record_ids[:, None]
    item_lengths = jnp.sum(jnp.where(record_pick, lengths[0][None, :], 0), axis=1)
    key_valid = jnp.arange(length, dtype=jnp.int32)[None, :] < item_lengths[:, None]
    query_grad, key_gradient, value_grad = lax.map(
        lambda group: item_backward(*group),
        (
            split_items(head_queries),
            split_items(head_keys),
            split_items(head_values),
            split_items(head_grads),
            key_valid,
        ),
    )
    query_back, key_backward, value_back = (
        lax.all_to_all(join_items(query_grad), "seq", split_axis=0, concat_axis=1, tiled=True),
        lax.all_to_all(join_items(key_gradient), "seq", split_axis=0, concat_axis=1, tiled=True),
        lax.all_to_all(join_items(value_grad), "seq", split_axis=0, concat_axis=1, tiled=True),
    )
    joined = jnp.concatenate(
        [
            query_back.reshape(frames * records, features),
            key_backward.reshape(frames * records, features),
            value_back.reshape(frames * records, features),
        ],
        axis=1,
    )
    norm_grad = lax.dot_general(
        joined,
        lax.all_gather(qkv_weight[0], "seq", axis=0, tiled=True),
        ROW_DOT,
        preferred_element_type=jnp.float32,
    )
    inputs = layer_input[0].reshape(frames * records, model_width).astype(jnp.float32)
    row_average = jnp.mean(inputs, axis=1, keepdims=True)
    centered_input = inputs - row_average
    var = jnp.mean(centered_input * centered_input, axis=1, keepdims=True)
    inverse_deviation = 1.0 / jnp.sqrt(var + EPSILON)
    normalized_input = centered_input * inverse_deviation
    scaled_rows = norm_grad * norm_gain[0][None, :]
    residual_branch = inverse_deviation * (
        scaled_rows
        - jnp.mean(scaled_rows, axis=1, keepdims=True)
        - normalized_input * jnp.mean(scaled_rows * normalized_input, axis=1, keepdims=True)
    )
    input_grad = (flat_grad.astype(jnp.float32) + residual_branch).astype(jnp.bfloat16)
    input_grad = input_grad.reshape(1, frames, records, model_width)
    return shifted(input_grad, "section", -1)


def body(
    dims,
    length_ref,
    li_ref,
    q_ref,
    k_ref,
    v_ref,
    og_ref,
    ow_in,
    w_in,
    gain_ref,
    out_ref,
    xq,
    xk,
    xv,
    xg,
    g_send,
    ow,
    w,
    joined,
    part_send,
    side_recv,
    sum_send,
    part_recv,
    li_here,
    og_here,
    x_send_sem,
    x_recv_sem,
    ow_send_sem,
    ow_side_sem,
    ow_recv_sem,
    w_send_sem,
    w_side_sem,
    w_near_sem,
    w_recv_sem,
    side_send_sem,
    side_recv_sem,
    p_send_sem,
    p_recv_sem,
    s_send_sem,
    s_recv_sem,
    local_sem,
):
    n, sections, groups, parts, frames, cols = dims
    pairs = cols // (2 * HS)
    section = lax.axis_index("section")
    me = lax.axis_index("seq")
    group = me // parts
    part = me % parts
    before = (section + sections - 1) % sections
    after = (section + 1) % sections

    def remote(src, dst, send, recv, sec, dev):
        return pltpu.make_async_remote_copy(
            src_ref=src,
            dst_ref=dst,
            send_sem=send,
            recv_sem=recv,
            device_id=(sec, dev),
            device_id_type=pl.DeviceIdType.MESH,
        )

    barrier = pltpu.get_barrier_semaphore()

    def greet(sec, dev):
        pl.semaphore_signal(
            barrier, inc=1, device_id=(sec, dev), device_id_type=pl.DeviceIdType.MESH
        )

    for k in range(1, n):
        greet(section, (me + k) % n)
    for k in range(n):
        greet(before, (me + k) % n)
        greet(after, (me + k) % n)

    heads = [(q_ref, xq), (k_ref, xk), (v_ref, xv), (g_send, xg)]

    def own(t):
        src, dst = heads[t]
        return pltpu.make_async_copy(
            src.at[group, :, pl.ds(pl.multiple_of(part * cols, cols), cols)],
            dst.at[me],
            local_sem.at[t],
        )

    def exchange(t, k):
        src, dst = heads[t]
        to = (me + k) % n
        return remote(
            src.at[to // parts, :, pl.ds(pl.multiple_of((to % parts) * cols, cols), cols)],
            dst.at[me],
            x_send_sem.at[t, k],
            x_recv_sem.at[t, k],
            section,
            to,
        )

    local_ow = pltpu.make_async_copy(ow_in, ow.at[me], local_sem.at[4])

    def piece(t, which):
        return w_in.at[:, pl.ds(pl.multiple_of((t * parts + which) * cols, cols), cols)]

    def local_w(t):
        return pltpu.make_async_copy(
            piece(t, part), w.at[me, :, pl.ds(t * cols, cols)], local_sem.at[5 + t]
        )

    local_ow.start()
    for t in range(3):
        local_w(t).start()
    for t in range(3):
        own(t).start()
    pl.semaphore_wait(barrier, 3 * n - 1)
    local_ow.wait()

    def ow_hop(slot, way, dev):
        return remote(
            ow.at[slot], ow.at[slot], ow_send_sem.at[way, slot], ow_recv_sem.at[slot], section, dev
        )

    def ow_side(slot, k):
        return remote(
            ow.at[slot],
            ow.at[slot],
            ow_side_sem.at[k, slot],
            ow_recv_sem.at[slot],
            section,
            group * parts + (part + k) % parts,
        )

    def w_hop(slot, way, dev):
        return remote(
            w.at[slot], w.at[slot], w_send_sem.at[way, slot], w_recv_sem.at[slot], section, dev
        )

    def w_side(t, k):
        other = (part + k) % parts
        return remote(
            piece(t, other),
            w.at[me, :, pl.ds(t * cols, cols)],
            w_side_sem.at[t, k],
            w_near_sem.at[t, k],
            section,
            group * parts + other,
        )

    def ways(origin, act):
        @pl.when((origin <= group) & (group + 1 < groups))
        def _():
            act(0, me + parts)

        @pl.when((origin >= group) & (group >= 1))
        def _():
            act(1, me - parts)

    def ow_pass(origin):
        slot = origin * parts + part
        ways(origin, lambda way, dev: ow_hop(slot, way, dev).start())
        for k in range(1, parts):
            ow_side(slot, k).start()

    def ow_arrive(origin):
        @pl.when((origin >= 0) & (origin < groups))
        def _():
            slot = origin * parts + part
            ow_hop(slot, 0, me).wait_recv()
            ow_pass(origin)

    def w_pass(origin):
        @pl.when((origin >= 0) & (origin < groups))
        def _():
            for other in range(parts):
                slot = origin * parts + other
                w_hop(slot, 0, me).wait_recv()
                ways(origin, lambda way, dev: w_hop(slot, way, dev).start())

    def w_first():
        for t in range(3):
            local_w(t).wait()
        ways(group, lambda way, dev: w_hop(me, way, dev).start())
        for k in range(1, parts):
            for t in range(3):
                w_side(t, k).wait_recv()
            slot = group * parts + (part + parts - k) % parts
            ways(group, lambda way, dev: w_hop(slot, way, dev).start())

    ow_pass(group)
    shift_og = remote(og_ref, og_here, s_send_sem.at[0], s_recv_sem.at[0], before, me)
    shift_li = remote(li_ref, li_here, s_send_sem.at[1], s_recv_sem.at[1], before, me)
    for k in range(1, n):
        exchange(0, k).start()
    shift_og.start()
    shift_li.start()
    for s in range(1, groups):
        ow_arrive(group - s)
        ow_arrive(group + s)
        if s == 1:
            for t in (1, 2):
                for k in range(1, n):
                    exchange(t, k).start()
    for k in range(1, parts):
        for t in range(3):
            w_side(t, k).start()
    for origin in range(groups):
        for k in range(1, parts):
            ow_side(origin * parts + (part + k) % parts, k).wait_recv()

    features = groups * parts
    rows_here = ow.shape[1]

    def project(i, carry):
        weight = ow[pl.ds(2 * i, 2)].reshape(2 * rows_here, ow.shape[2])
        result = lax.dot_general(
            og_ref[...], weight, ROW_DOT, preferred_element_type=jnp.float32
        ).astype(jnp.bfloat16)
        g_send[:, :, pl.ds(pl.multiple_of(i * 2 * rows_here, 2 * rows_here), 2 * rows_here)] = (
            result.reshape(groups, frames, 2 * rows_here)
        )
        return carry

    lax.fori_loop(0, features // 2, project, 0)
    own(3).start()
    for k in range(1, n):
        exchange(3, k).start()
    w_first()
    for t in range(4):
        own(t).wait()
        for k in range(1, n):
            exchange(t, k).wait_recv()

    length = n * frames
    valid = length_ref[0]
    keys_ok = lax.broadcasted_iota(jnp.int32, (length, 1), 0) < valid
    low_lanes = lax.broadcasted_iota(jnp.int32, (length, 2 * HS), 1) < HS
    scale = HS ** (-0.5)

    def attend(j, carry):
        lanes = pl.ds(pl.multiple_of(j * 2 * HS, 2 * HS), 2 * HS)
        queries, keys, values, grads = (
            x[:, :, lanes].reshape(length, 2 * HS) for x in (xq, xk, xv, xg)
        )
        keys_across = keys.T
        nothing = jnp.zeros_like(keys)
        halves = []
        for h in range(2):
            mine = low_lanes if h == 0 else jnp.logical_not(low_lanes)
            key_h = jnp.where(mine, keys, nothing)
            value_h = jnp.where(mine, values, nothing)
            scores = (
                lax.dot_general(key_h, queries, ROW_DOT, preferred_element_type=jnp.float32)
                * scale
            )
            scores = jnp.where(keys_ok, scores, MASKED)
            weights = jnp.exp(scores - jnp.max(scores, axis=0, keepdims=True))
            probs = weights * (1.0 / jnp.sum(weights, axis=0, keepdims=True))
            grad_probs = lax.dot_general(
                value_h, grads, ROW_DOT, preferred_element_type=jnp.float32
            )
            centre = jnp.sum(probs * grad_probs, axis=0, keepdims=True)
            grad_scores = (probs * (grad_probs - centre)).astype(jnp.bfloat16)
            value_grad = jnp.dot(
                probs.astype(jnp.bfloat16), grads, preferred_element_type=jnp.float32
            )
            key_grad = jnp.dot(grad_scores, queries, preferred_element_type=jnp.float32)
            query_grad = jnp.dot(
                keys_across[h * HS : (h + 1) * HS], grad_scores, preferred_element_type=jnp.float32
            )
            halves.append((query_grad, key_grad, value_grad))
        (query_0, key_0, value_0), (query_1, key_1, value_1) = halves
        query_both = (jnp.concatenate([query_0, query_1], axis=0) * scale).T
        key_both = jnp.where(low_lanes, key_0, key_1) * scale
        value_both = jnp.where(low_lanes, value_0, value_1)
        for t, both in enumerate((query_both, key_both, value_both)):
            at = pl.multiple_of(t * cols + j * 2 * HS, 2 * HS)
            joined[:, pl.ds(at, 2 * HS)] = both.astype(jnp.bfloat16)

        @pl.when(j == pairs - 2)
        def _():
            w_pass(group - 1)
            w_pass(group + 1)

        return carry

    if pairs < 2:
        w_pass(group - 1)
        w_pass(group + 1)
    lax.fori_loop(0, pairs, attend, 0)

    def side_copy(origin, k):
        other = (part + k) % parts
        return remote(
            part_send.at[origin, other],
            side_recv.at[origin, k],
            side_send_sem.at[origin, k],
            side_recv_sem.at[origin, k],
            section,
            group * parts + other,
        )

    def sum_copy(origin, to):
        return remote(
            sum_send.at[origin, to],
            part_recv.at[group, origin],
            p_send_sem.at[origin, to],
            p_recv_sem.at[group, origin],
            before,
            to * parts + part,
        )

    blocks = 2 * groups - 1

    def origin_of(i):
        return group + ((i + 1) // 2) * (1 - 2 * (i % 2))

    def norm_block(i, carry):
        earlier = origin_of(i - 2)

        @pl.when((i >= 2) & (earlier >= 0) & (earlier < groups))
        def _():
            total = part_send[earlier, part].astype(jnp.float32)
            for k in range(1, parts):
                side_copy(earlier, k).wait_recv()
                total = total + side_recv[earlier, k].astype(jnp.float32)
            sum_send[earlier] = total.astype(jnp.bfloat16)
            for k in range(groups):
                sum_copy(earlier, (group + k) % groups).start()

        origin = origin_of(i)

        @pl.when((i >= 3) & (i < blocks))
        def _():
            w_pass(origin)

        @pl.when((i < blocks) & (origin >= 0) & (origin < groups))
        def _():
            weight = w[pl.ds(origin * parts, parts)].reshape(parts * w.shape[1], w.shape[2])
            sums = lax.dot_general(
                joined[...], weight, ROW_DOT, preferred_element_type=jnp.float32
            )
            sums = (sums * gain_ref[origin]).astype(jnp.bfloat16)
            sums = sums.reshape(groups, parts, frames, sums.shape[1])
            for other in range(parts):
                part_send[origin, other] = sums[:, other]
            for k in range(1, parts):
                side_copy(origin, k).start()

        return carry

    lax.fori_loop(0, blocks + 2, norm_block, 0)

    shift_og.wait_recv()
    shift_li.wait_recv()
    for src in range(groups):
        for origin in range(groups):
            remote(
                sum_send.at[origin, 0],
                part_recv.at[src, origin],
                p_send_sem.at[origin, 0],
                p_recv_sem.at[src, origin],
                before,
                me,
            ).wait_recv()

    width = li_here.shape[1]

    def finish(r, carry):
        rows = pl.ds(pl.multiple_of(r * frames, frames), frames)
        inputs = li_here[rows, :].astype(jnp.float32)
        centered = inputs - jnp.sum(inputs, axis=1, keepdims=True) * (1.0 / width)
        var = jnp.sum(centered * centered, axis=1, keepdims=True) * (1.0 / width)
        deviation = 1.0 / jnp.sqrt(var + EPSILON)
        normal = centered * deviation
        scaled = []
        for origin in range(groups):
            scaled.append(part_recv[r, origin].astype(jnp.float32))
        scaled = jnp.concatenate(scaled, axis=1)
        average = jnp.sum(scaled, axis=1, keepdims=True) * (1.0 / width)
        along = jnp.sum(scaled * normal, axis=1, keepdims=True) * (1.0 / width)
        branch = deviation * (scaled - average - normal * along)
        out_ref[rows, :] = (og_here[rows, :].astype(jnp.float32) + branch).astype(jnp.bfloat16)
        return carry

    lax.fori_loop(0, groups, finish, 0)

    for t in range(4):
        for k in range(1, n):
            exchange(t, k).wait_send()
    for origin in range(groups):
        slot = origin * parts + part
        ways(origin, lambda way, dev: ow_hop(slot, way, dev).wait_send())
        for k in range(1, parts):
            ow_side(slot, k).wait_send()
        for other in range(parts):
            w_slot = origin * parts + other
            ways(origin, lambda way, dev: w_hop(w_slot, way, dev).wait_send())
        for to in range(groups):
            sum_copy(origin, to).wait_send()
        for k in range(1, parts):
            side_copy(origin, k).wait_send()
    for k in range(1, parts):
        for t in range(3):
            w_side(t, k).wait_send()
    shift_og.wait_send()
    shift_li.wait_send()


def on_device_fused(
    layer_input,
    norm_gain,
    queries,
    key_states,
    value_states,
    out_grad,
    out_weight,
    qkv_weight,
    lengths,
):
    n = lax.axis_size("seq")
    sections = lax.axis_size("section")
    frames, records, features = queries.shape[1:]
    width = out_grad.shape[3]
    parts = n // records
    cols = features // parts
    ow_rows = out_weight.shape[1]
    w_rows = qkv_weight.shape[1]
    block = parts * w_rows
    group = lax.axis_index("seq") // parts
    length_here = lax.dynamic_slice(lengths[0], (group,), (1,))

    def by_record(x):
        return x[0].transpose(1, 0, 2)

    flat_input = by_record(layer_input).reshape(records * frames, width)
    flat_grad = by_record(out_grad).reshape(records * frames, width)
    gain = norm_gain[0].reshape(records, 1, block)
    vmem = pl.BlockSpec(memory_space=pltpu.VMEM)
    low = jnp.bfloat16
    dma = pltpu.SemaphoreType.DMA
    out = pl.pallas_call(
        functools.partial(body, (n, sections, records, parts, frames, cols)),
        out_shape=jax.ShapeDtypeStruct((records * frames, width), low),
        in_specs=[pl.BlockSpec(memory_space=pltpu.SMEM)] + [vmem] * 8,
        out_specs=vmem,
        scratch_shapes=[pltpu.VMEM((n, frames, cols), low)] * 4
        + [
            pltpu.VMEM((records, frames, features), low),
            pltpu.VMEM((n, ow_rows, width), low),
            pltpu.VMEM((n, w_rows, 3 * cols), low),
            pltpu.VMEM((n * frames, 3 * cols), low),
            pltpu.VMEM((records, parts, records, frames, block), low),
            pltpu.VMEM((records, parts, records, frames, block), low),
            pltpu.VMEM((records, records, frames, block), low),
            pltpu.VMEM((records, records, frames, block), low),
            pltpu.VMEM((records * frames, width), low),
            pltpu.VMEM((records * frames, width), low),
            dma((4, n)),
            dma((4, n)),
            dma((2, n)),
            dma((parts, n)),
            dma((n,)),
            dma((2, n)),
            dma((3, parts)),
            dma((3, parts)),
            dma((n,)),
            dma((records, parts)),
            dma((records, parts)),
            dma((records, records)),
            dma((records, records)),
            dma((2,)),
            dma((2,)),
            dma((8,)),
        ],
        compiler_params=pltpu.CompilerParams(
            collective_id=0, has_side_effects=True, vmem_limit_bytes=60 * 1024 * 1024
        ),
    )(
        length_here,
        flat_input,
        by_record(queries),
        by_record(key_states),
        by_record(value_states),
        flat_grad,
        out_weight[0],
        qkv_weight[0],
        gain,
    )
    return out.reshape(records, frames, width).transpose(1, 0, 2)[None]


def fits(mesh, records, features):
    n = mesh.shape["seq"]
    if n % records or mesh.shape["section"] < 2:
        return False
    parts = n // records
    return features % (parts * 2 * HS) == 0 and n % 2 == 0


def solution(mesh):
    in_specs = (
        P("section", "seq", None, None),
        P("section", None),
        P("section", "seq", None, None),
        P("section", "seq", None, None),
        P("section", "seq", None, None),
        P("section", "seq", None, None),
        P("section", "seq", None),
        P("section", "seq", None),
        P("section", None),
    )
    out_specs = P("section", "seq", None, None)

    def run(*arrays):
        fused = fits(mesh, arrays[2].shape[2], arrays[2].shape[3])
        return jax.shard_map(
            on_device_fused if fused else on_device,
            mesh=mesh,
            in_specs=in_specs,
            out_specs=out_specs,
            check_vma=False,
        )(*arrays)

    return run
```

```python
import functools

import jax
import jax.numpy as jnp
from jax import lax
from jax.experimental import pallas as pl
from jax.experimental.pallas import tpu as pltpu
from jax.sharding import PartitionSpec as P

HEADS = 16
HS = 64


EPSILON = 1e-05
MASKED = -1e30
ROW_DOT = (((1,), (1,)), ((), ()))
COL_DOT = (((0,), (0,)), ((), ()))


def shifted(shard, axis, by):
    count = lax.axis_size(axis)
    return lax.ppermute(shard, axis, [(i, (i + by) % count) for i in range(count)])


def item_backward(query_rows, key_rows, value_rows, grad_rows, key_valid):
    length = query_rows.shape[0]
    block = min(512, length)
    scale = HS ** (-0.5)
    offsets = jnp.arange(0, length, block)
    zeros = jnp.zeros((length, query_rows.shape[1]), jnp.float32)

    def step(carry, offset):
        key_total, value_total = carry
        query_block = lax.dynamic_slice_in_dim(query_rows, offset, block, 0)
        grad_block = lax.dynamic_slice_in_dim(grad_rows, offset, block, 0)
        scores = (
            lax.dot_general(query_block, key_rows, ROW_DOT, preferred_element_type=jnp.float32)
            * scale
        )
        scores = jnp.where(key_valid[None, :], scores, MASKED)
        largest = jnp.max(scores, axis=1, keepdims=True)
        weights = jnp.exp(scores - largest)
        probs = weights / jnp.sum(weights, axis=1, keepdims=True)
        probs_low = probs.astype(jnp.bfloat16)
        grad_probs = lax.dot_general(
            grad_block, value_rows, ROW_DOT, preferred_element_type=jnp.float32
        )
        centre = jnp.sum(probs * grad_probs, axis=1, keepdims=True)
        grad_scores = (probs * (grad_probs - centre) * scale).astype(jnp.bfloat16)
        query_grad = jnp.dot(grad_scores, key_rows, preferred_element_type=jnp.float32)
        key_total = key_total + lax.dot_general(
            grad_scores, query_block, COL_DOT, preferred_element_type=jnp.float32
        )
        value_total = value_total + lax.dot_general(
            probs_low, grad_block, COL_DOT, preferred_element_type=jnp.float32
        )
        return ((key_total, value_total), query_grad.astype(jnp.bfloat16))

    (key_total, value_total), query_parts = lax.scan(step, (zeros, zeros), offsets)
    query_grad = query_parts.reshape(length, query_rows.shape[1])
    return (query_grad, key_total.astype(jnp.bfloat16), value_total.astype(jnp.bfloat16))


def split_items(columns):
    length = columns.shape[0]
    count = columns.shape[1] // HS
    return columns.reshape(length, count, HS).transpose(1, 0, 2)


def join_items(items):
    count = items.shape[0]
    length = items.shape[1]
    return items.transpose(1, 0, 2).reshape(length, count * HS)


def project_grad(flat_grad, out_rows):
    return lax.dot_general(
        flat_grad,
        lax.all_gather(out_rows, "seq", axis=0, tiled=True),
        ROW_DOT,
        preferred_element_type=jnp.float32,
    ).astype(jnp.bfloat16)


def on_device(
    layer_input,
    norm_gain,
    queries,
    key_states,
    value_states,
    out_grad,
    out_weight,
    qkv_weight,
    lengths,
):
    frames = queries.shape[1]
    records = queries.shape[2]
    features = queries.shape[3]
    model_width = out_grad.shape[3]
    flat_grad = out_grad[0].reshape(frames * records, model_width)
    frame_queries = queries[0].reshape(frames, records * features)
    frame_keys = key_states[0].reshape(frames, records * features)
    frame_values = value_states[0].reshape(frames, records * features)
    attn_grad = project_grad(flat_grad, out_weight[0])
    head_queries, head_keys, head_values, head_grads = (
        lax.all_to_all(frame_queries, "seq", split_axis=1, concat_axis=0, tiled=True),
        lax.all_to_all(frame_keys, "seq", split_axis=1, concat_axis=0, tiled=True),
        lax.all_to_all(frame_values, "seq", split_axis=1, concat_axis=0, tiled=True),
        lax.all_to_all(
            attn_grad.reshape(frames, records * features),
            "seq",
            split_axis=1,
            concat_axis=0,
            tiled=True,
        ),
    )
    items_here = head_queries.shape[1] // HS
    length = head_queries.shape[0]
    item_ids = lax.axis_index("seq") * items_here + jnp.arange(items_here, dtype=jnp.int32)
    record_ids = item_ids // HEADS
    record_pick = jnp.arange(records, dtype=jnp.int32)[None, :] == record_ids[:, None]
    item_lengths = jnp.sum(jnp.where(record_pick, lengths[0][None, :], 0), axis=1)
    key_valid = jnp.arange(length, dtype=jnp.int32)[None, :] < item_lengths[:, None]
    query_grad, key_gradient, value_grad = lax.map(
        lambda group: item_backward(*group),
        (
            split_items(head_queries),
            split_items(head_keys),
            split_items(head_values),
            split_items(head_grads),
            key_valid,
        ),
    )
    query_back, key_backward, value_back = (
        lax.all_to_all(join_items(query_grad), "seq", split_axis=0, concat_axis=1, tiled=True),
        lax.all_to_all(join_items(key_gradient), "seq", split_axis=0, concat_axis=1, tiled=True),
        lax.all_to_all(join_items(value_grad), "seq", split_axis=0, concat_axis=1, tiled=True),
    )
    joined = jnp.concatenate(
        [
            query_back.reshape(frames * records, features),
            key_backward.reshape(frames * records, features),
            value_back.reshape(frames * records, features),
        ],
        axis=1,
    )
    norm_grad = lax.dot_general(
        joined,
        lax.all_gather(qkv_weight[0], "seq", axis=0, tiled=True),
        ROW_DOT,
        preferred_element_type=jnp.float32,
    )
    inputs = layer_input[0].reshape(frames * records, model_width).astype(jnp.float32)
    row_average = jnp.mean(inputs, axis=1, keepdims=True)
    centered_input = inputs - row_average
    var = jnp.mean(centered_input * centered_input, axis=1, keepdims=True)
    inverse_deviation = 1.0 / jnp.sqrt(var + EPSILON)
    normalized_input = centered_input * inverse_deviation
    scaled_rows = norm_grad * norm_gain[0][None, :]
    residual_branch = inverse_deviation * (
        scaled_rows
        - jnp.mean(scaled_rows, axis=1, keepdims=True)
        - normalized_input * jnp.mean(scaled_rows * normalized_input, axis=1, keepdims=True)
    )
    input_grad = (flat_grad.astype(jnp.float32) + residual_branch).astype(jnp.bfloat16)
    input_grad = input_grad.reshape(1, frames, records, model_width)
    return shifted(input_grad, "section", -1)


def body(
    dims,
    length_ref,
    li_ref,
    q_ref,
    k_ref,
    v_ref,
    og_ref,
    ow_in,
    w_in,
    gain_ref,
    out_ref,
    xq,
    xk,
    xv,
    xg,
    g_send,
    ow,
    w,
    joined,
    part_send,
    side_recv,
    sum_send,
    part_recv,
    li_here,
    og_here,
    x_send_sem,
    x_recv_sem,
    ow_send_sem,
    ow_side_sem,
    ow_recv_sem,
    w_send_sem,
    w_side_sem,
    w_near_sem,
    w_recv_sem,
    side_send_sem,
    side_recv_sem,
    p_send_sem,
    p_recv_sem,
    s_send_sem,
    s_recv_sem,
    local_sem,
):
    n, sections, groups, parts, frames, cols = dims
    pairs = cols // (2 * HS)
    section = lax.axis_index("section")
    me = lax.axis_index("seq")
    group = me // parts
    part = me % parts
    before = (section + sections - 1) % sections
    after = (section + 1) % sections

    def remote(src, dst, send, recv, sec, dev):
        return pltpu.make_async_remote_copy(
            src_ref=src,
            dst_ref=dst,
            send_sem=send,
            recv_sem=recv,
            device_id=(sec, dev),
            device_id_type=pl.DeviceIdType.MESH,
        )

    barrier = pltpu.get_barrier_semaphore()

    def greet(sec, dev):
        pl.semaphore_signal(
            barrier, inc=1, device_id=(sec, dev), device_id_type=pl.DeviceIdType.MESH
        )

    for k in range(1, n):
        greet(section, (me + k) % n)
    for k in range(n):
        greet(before, (me + k) % n)
        greet(after, (me + k) % n)

    heads = [(q_ref, xq), (k_ref, xk), (v_ref, xv), (g_send, xg)]

    def own(t):
        src, dst = heads[t]
        return pltpu.make_async_copy(
            src.at[group, :, pl.ds(pl.multiple_of(part * cols, cols), cols)],
            dst.at[me],
            local_sem.at[t],
        )

    def exchange(t, k):
        src, dst = heads[t]
        to = (me + k) % n
        return remote(
            src.at[to // parts, :, pl.ds(pl.multiple_of((to % parts) * cols, cols), cols)],
            dst.at[me],
            x_send_sem.at[t, k],
            x_recv_sem.at[t, k],
            section,
            to,
        )

    local_ow = pltpu.make_async_copy(ow_in, ow.at[me], local_sem.at[4])

    def piece(t, which):
        return w_in.at[:, pl.ds(pl.multiple_of((t * parts + which) * cols, cols), cols)]

    def local_w(t):
        return pltpu.make_async_copy(
            piece(t, part), w.at[me, :, pl.ds(t * cols, cols)], local_sem.at[5 + t]
        )

    local_ow.start()
    for t in range(3):
        local_w(t).start()
    for t in range(3):
        own(t).start()
    pl.semaphore_wait(barrier, 3 * n - 1)
    local_ow.wait()

    def ow_hop(slot, way, dev):
        return remote(
            ow.at[slot], ow.at[slot], ow_send_sem.at[way, slot], ow_recv_sem.at[slot], section, dev
        )

    def ow_side(slot, k):
        return remote(
            ow.at[slot],
            ow.at[slot],
            ow_side_sem.at[k, slot],
            ow_recv_sem.at[slot],
            section,
            group * parts + (part + k) % parts,
        )

    def w_hop(slot, way, dev):
        return remote(
            w.at[slot], w.at[slot], w_send_sem.at[way, slot], w_recv_sem.at[slot], section, dev
        )

    def w_side(t, k):
        other = (part + k) % parts
        return remote(
            piece(t, other),
            w.at[me, :, pl.ds(t * cols, cols)],
            w_side_sem.at[t, k],
            w_near_sem.at[t, k],
            section,
            group * parts + other,
        )

    def ways(origin, act):
        @pl.when((origin <= group) & (group + 1 < groups))
        def _():
            act(0, me + parts)

        @pl.when((origin >= group) & (group >= 1))
        def _():
            act(1, me - parts)

    def ow_pass(origin):
        slot = origin * parts + part
        ways(origin, lambda way, dev: ow_hop(slot, way, dev).start())
        for k in range(1, parts):
            ow_side(slot, k).start()

    def ow_arrive(origin):
        @pl.when((origin >= 0) & (origin < groups))
        def _():
            slot = origin * parts + part
            ow_hop(slot, 0, me).wait_recv()
            ow_pass(origin)

    def w_pass(origin):
        @pl.when((origin >= 0) & (origin < groups))
        def _():
            for other in range(parts):
                slot = origin * parts + other
                w_hop(slot, 0, me).wait_recv()
                ways(origin, lambda way, dev: w_hop(slot, way, dev).start())

    def w_first():
        for t in range(3):
            local_w(t).wait()
        ways(group, lambda way, dev: w_hop(me, way, dev).start())
        for k in range(1, parts):
            for t in range(3):
                w_side(t, k).wait_recv()
            slot = group * parts + (part + parts - k) % parts
            ways(group, lambda way, dev: w_hop(slot, way, dev).start())

    ow_pass(group)
    shift_og = remote(og_ref, og_here, s_send_sem.at[0], s_recv_sem.at[0], before, me)
    shift_li = remote(li_ref, li_here, s_send_sem.at[1], s_recv_sem.at[1], before, me)
    for k in range(1, n):
        exchange(0, k).start()
    shift_og.start()
    shift_li.start()
    for s in range(1, groups):
        ow_arrive(group - s)
        ow_arrive(group + s)
    for k in range(1, parts):
        for t in range(3):
            w_side(t, k).start()
    for t in (1, 2):
        for k in range(1, n):
            exchange(t, k).start()
    w_first()
    for origin in range(groups):
        for k in range(1, parts):
            ow_side(origin * parts + (part + k) % parts, k).wait_recv()

    features = groups * parts
    rows_here = ow.shape[1]

    def project(i, carry):
        weight = ow[pl.ds(2 * i, 2)].reshape(2 * rows_here, ow.shape[2])
        result = lax.dot_general(
            og_ref[...], weight, ROW_DOT, preferred_element_type=jnp.float32
        ).astype(jnp.bfloat16)
        g_send[:, :, pl.ds(pl.multiple_of(i * 2 * rows_here, 2 * rows_here), 2 * rows_here)] = (
            result.reshape(groups, frames, 2 * rows_here)
        )
        return carry

    lax.fori_loop(0, features // 2, project, 0)
    own(3).start()
    for k in range(1, n):
        exchange(3, k).start()
    w_pass(group - 1)
    w_pass(group + 1)
    for t in range(4):
        own(t).wait()
        for k in range(1, n):
            exchange(t, k).wait_recv()

    length = n * frames
    valid = length_ref[0]
    keys_ok = lax.broadcasted_iota(jnp.int32, (length, 1), 0) < valid
    low_lanes = lax.broadcasted_iota(jnp.int32, (length, 2 * HS), 1) < HS
    scale = HS ** (-0.5)

    def attend(j, carry):
        lanes = pl.ds(pl.multiple_of(j * 2 * HS, 2 * HS), 2 * HS)
        queries, keys, values, grads = (
            x[:, :, lanes].reshape(length, 2 * HS) for x in (xq, xk, xv, xg)
        )
        keys_across = keys.T
        nothing = jnp.zeros_like(keys)
        halves = []
        for h in range(2):
            mine = low_lanes if h == 0 else jnp.logical_not(low_lanes)
            key_h = jnp.where(mine, keys, nothing)
            value_h = jnp.where(mine, values, nothing)
            scores = (
                lax.dot_general(key_h, queries, ROW_DOT, preferred_element_type=jnp.float32)
                * scale
            )
            scores = jnp.where(keys_ok, scores, MASKED)
            weights = jnp.exp(scores - jnp.max(scores, axis=0, keepdims=True))
            probs = weights * (1.0 / jnp.sum(weights, axis=0, keepdims=True))
            grad_probs = lax.dot_general(
                value_h, grads, ROW_DOT, preferred_element_type=jnp.float32
            )
            centre = jnp.sum(probs * grad_probs, axis=0, keepdims=True)
            grad_scores = (probs * (grad_probs - centre)).astype(jnp.bfloat16)
            value_grad = jnp.dot(
                probs.astype(jnp.bfloat16), grads, preferred_element_type=jnp.float32
            )
            key_grad = jnp.dot(grad_scores, queries, preferred_element_type=jnp.float32)
            query_grad = jnp.dot(
                keys_across[h * HS : (h + 1) * HS], grad_scores, preferred_element_type=jnp.float32
            )
            halves.append((query_grad, key_grad, value_grad))
        (query_0, key_0, value_0), (query_1, key_1, value_1) = halves
        query_both = (jnp.concatenate([query_0, query_1], axis=0) * scale).T
        key_both = jnp.where(low_lanes, key_0, key_1) * scale
        value_both = jnp.where(low_lanes, value_0, value_1)
        for t, both in enumerate((query_both, key_both, value_both)):
            at = pl.multiple_of(t * cols + j * 2 * HS, 2 * HS)
            joined[:, pl.ds(at, 2 * HS)] = both.astype(jnp.bfloat16)

        @pl.when(j == pairs - 2)
        def _():
            w_pass(group - 2)
            w_pass(group + 2)

        return carry

    if pairs < 2:
        w_pass(group - 2)
        w_pass(group + 2)
    lax.fori_loop(0, pairs, attend, 0)

    def side_copy(origin, k):
        other = (part + k) % parts
        return remote(
            part_send.at[origin, other],
            side_recv.at[origin, k],
            side_send_sem.at[origin, k],
            side_recv_sem.at[origin, k],
            section,
            group * parts + other,
        )

    def sum_copy(origin, to):
        return remote(
            sum_send.at[origin, to],
            part_recv.at[group, origin],
            p_send_sem.at[origin, to],
            p_recv_sem.at[group, origin],
            before,
            to * parts + part,
        )

    blocks = 2 * groups - 1

    def origin_of(i):
        return group + ((i + 1) // 2) * (1 - 2 * (i % 2))

    def norm_block(i, carry):
        earlier = origin_of(i - 2)

        @pl.when((i >= 2) & (earlier >= 0) & (earlier < groups))
        def _():
            total = part_send[earlier, part].astype(jnp.float32)
            for k in range(1, parts):
                side_copy(earlier, k).wait_recv()
                total = total + side_recv[earlier, k].astype(jnp.float32)
            sum_send[earlier] = total.astype(jnp.bfloat16)
            for k in range(groups):
                sum_copy(earlier, (group + k) % groups).start()

        origin = origin_of(i)

        @pl.when((i >= 5) & (i < blocks))
        def _():
            w_pass(origin)

        @pl.when((i < blocks) & (origin >= 0) & (origin < groups))
        def _():
            weight = w[pl.ds(origin * parts, parts)].reshape(parts * w.shape[1], w.shape[2])
            sums = lax.dot_general(
                joined[...], weight, ROW_DOT, preferred_element_type=jnp.float32
            )
            sums = (sums * gain_ref[origin]).astype(jnp.bfloat16)
            sums = sums.reshape(groups, parts, frames, sums.shape[1])
            for other in range(parts):
                part_send[origin, other] = sums[:, other]
            for k in range(1, parts):
                side_copy(origin, k).start()

        return carry

    lax.fori_loop(0, blocks + 2, norm_block, 0)

    shift_og.wait_recv()
    shift_li.wait_recv()
    for src in range(groups):
        for origin in range(groups):
            remote(
                sum_send.at[origin, 0],
                part_recv.at[src, origin],
                p_send_sem.at[origin, 0],
                p_recv_sem.at[src, origin],
                before,
                me,
            ).wait_recv()

    width = og_here.shape[1]

    def finish(r):
        rows = pl.ds(r * frames, frames)
        inputs = li_here[:, r, :].astype(jnp.float32)
        centered = inputs - jnp.sum(inputs, axis=1, keepdims=True) * (1.0 / width)
        var = jnp.sum(centered * centered, axis=1, keepdims=True) * (1.0 / width)
        deviation = 1.0 / jnp.sqrt(var + EPSILON)
        normal = centered * deviation
        scaled = []
        for origin in range(groups):
            scaled.append(part_recv[r, origin].astype(jnp.float32))
        scaled = jnp.concatenate(scaled, axis=1)
        average = jnp.sum(scaled, axis=1, keepdims=True) * (1.0 / width)
        along = jnp.sum(scaled * normal, axis=1, keepdims=True) * (1.0 / width)
        branch = deviation * (scaled - average - normal * along)
        out_ref[rows, :] = (og_here[rows, :].astype(jnp.float32) + branch).astype(jnp.bfloat16)

    for r in range(groups):
        finish(r)

    for t in range(4):
        for k in range(1, n):
            exchange(t, k).wait_send()
    for origin in range(groups):
        slot = origin * parts + part
        ways(origin, lambda way, dev: ow_hop(slot, way, dev).wait_send())
        for k in range(1, parts):
            ow_side(slot, k).wait_send()
        for other in range(parts):
            w_slot = origin * parts + other
            ways(origin, lambda way, dev: w_hop(w_slot, way, dev).wait_send())
        for to in range(groups):
            sum_copy(origin, to).wait_send()
        for k in range(1, parts):
            side_copy(origin, k).wait_send()
    for k in range(1, parts):
        for t in range(3):
            w_side(t, k).wait_send()
    shift_og.wait_send()
    shift_li.wait_send()


def on_device_fused(
    layer_input,
    norm_gain,
    queries,
    key_states,
    value_states,
    out_grad,
    out_weight,
    qkv_weight,
    lengths,
):
    n = lax.axis_size("seq")
    sections = lax.axis_size("section")
    frames, records, features = queries.shape[1:]
    width = out_grad.shape[3]
    parts = n // records
    cols = features // parts
    ow_rows = out_weight.shape[1]
    w_rows = qkv_weight.shape[1]
    block = parts * w_rows
    group = lax.axis_index("seq") // parts
    length_here = lax.dynamic_slice(lengths[0], (group,), (1,))

    def by_record(x):
        return x[0].transpose(1, 0, 2)

    flat_input = layer_input[0]
    flat_grad = by_record(out_grad).reshape(records * frames, width)
    gain = norm_gain[0].reshape(records, 1, block)
    vmem = pl.BlockSpec(memory_space=pltpu.VMEM)
    low = jnp.bfloat16
    dma = pltpu.SemaphoreType.DMA
    out = pl.pallas_call(
        functools.partial(body, (n, sections, records, parts, frames, cols)),
        out_shape=jax.ShapeDtypeStruct((records * frames, width), low),
        in_specs=[pl.BlockSpec(memory_space=pltpu.SMEM)] + [vmem] * 8,
        out_specs=vmem,
        scratch_shapes=[pltpu.VMEM((n, frames, cols), low)] * 4
        + [
            pltpu.VMEM((records, frames, features), low),
            pltpu.VMEM((n, ow_rows, width), low),
            pltpu.VMEM((n, w_rows, 3 * cols), low),
            pltpu.VMEM((n * frames, 3 * cols), low),
            pltpu.VMEM((records, parts, records, frames, block), low),
            pltpu.VMEM((records, parts, records, frames, block), low),
            pltpu.VMEM((records, records, frames, block), low),
            pltpu.VMEM((records, records, frames, block), low),
            pltpu.VMEM((frames, records, width), low),
            pltpu.VMEM((records * frames, width), low),
            dma((4, n)),
            dma((4, n)),
            dma((2, n)),
            dma((parts, n)),
            dma((n,)),
            dma((2, n)),
            dma((3, parts)),
            dma((3, parts)),
            dma((n,)),
            dma((records, parts)),
            dma((records, parts)),
            dma((records, records)),
            dma((records, records)),
            dma((2,)),
            dma((2,)),
            dma((8,)),
        ],
        compiler_params=pltpu.CompilerParams(
            collective_id=0, has_side_effects=True, vmem_limit_bytes=60 * 1024 * 1024
        ),
    )(
        length_here,
        flat_input,
        by_record(queries),
        by_record(key_states),
        by_record(value_states),
        flat_grad,
        out_weight[0],
        qkv_weight[0],
        gain,
    )
    return out.reshape(records, frames, width).transpose(1, 0, 2)[None]


def fits(mesh, records, features):
    n = mesh.shape["seq"]
    if n % records or mesh.shape["section"] < 2:
        return False
    parts = n // records
    return features % (parts * 2 * HS) == 0 and n % 2 == 0


def solution(mesh):
    in_specs = (
        P("section", "seq", None, None),
        P("section", None),
        P("section", "seq", None, None),
        P("section", "seq", None, None),
        P("section", "seq", None, None),
        P("section", "seq", None, None),
        P("section", "seq", None),
        P("section", "seq", None),
        P("section", None),
    )
    out_specs = P("section", "seq", None, None)

    def run(*arrays):
        fused = fits(mesh, arrays[2].shape[2], arrays[2].shape[3])
        return jax.shard_map(
            on_device_fused if fused else on_device,
            mesh=mesh,
            in_specs=in_specs,
            out_specs=out_specs,
            check_vma=False,
        )(*arrays)

    return run
```
